512 devices in a mesh: space: 64 (over z, y), batch: 8 (over x, core).
Axes of the slice: x: 4, y: 8, z: 8, core: 2. Of those that a mesh axis runs over, the one named last changes fastest.
Arguments:
- features: bfloat16 [8, 32768, 128], P('batch', 'space'), may hold values from -6 to 6
- weights: bfloat16 [27, 128, 128], replicated, may hold values from -0.109375 to 0.109375
- kernel_map: int32 [8, 27, 32768], P('batch', None, 'space'), may hold values from 0 to 768, as said below
- send_rows: int32 [8, 2, 8192], P('batch', None, 'space'), may hold values from 0 to 511, as said below
- counts: int32 [8, 64], P('batch', 'space'), may hold values from 64 to 512, as said below
- cotangent: bfloat16 [8, 32768, 128], P('batch', 'space'), may hold values from -6 to 6
Outputs:
- output: bfloat16 [8, 32768, 128], P('batch', 'space')
- grad_features: bfloat16 [8, 32768, 128], P('batch', 'space')
- grad_weights: float32 [27, 128, 128], replicated
The draws below stay inside these ranges and needn't reach their ends.
Inputs may be any that keep to these rules, and one draw needn't show every extreme that they name: `kernel_map`: values below 512 are active slots of the same block (below its count); 512 to 639 are rows received from the lower block, the next 128 rows from the upper block, 768 is the zero row. The first block never reads the lower rows, the last never the upper ones. The middle offset reads each active slot itself; inactive slots read only the zero row. `send_rows`: every entry is an active slot of the sending block. `counts`: each scene tile has a block with all 512 slots active and a block with exactly 64; every block has at least 64.
All inputs are finite; a program needn't handle non-finite values.
Results may differ from the reference program's by a relative error of at most 0.001.
Values may be sent and summed in bfloat16 or wider, within the bound.
No kernel may reach another device: no remote copies, remote signals or barrier semaphores. Data moves between devices by JAX's collectives and lax.ppermute only.
A program may use at most 64 MiB of HBM per device.

```python
import jax
import jax.numpy as jnp
from jax import lax

C = 128
KV = 27
VOX = 512
HALO = 128
ROWS = 32768
SCENES = 8
N_SPACE = 64


def geometry(key):
    blocks = ROWS // VOX
    counts = jax.random.randint(jax.random.fold_in(key, 11), (SCENES, blocks), VOX // 8, VOX + 1)
    full_block = jax.random.randint(jax.random.fold_in(key, 12), (SCENES, 1), 0, blocks)
    small_block = (full_block + 1) % blocks
    block_line = jnp.arange(blocks)[None, :]
    counts = jnp.where(block_line == small_block, VOX // 8, counts)
    counts = jnp.where(block_line == full_block, VOX, counts).astype(jnp.int32)
    drawn_rows = jax.random.randint(jax.random.fold_in(key, 13), (SCENES, 2, blocks, HALO), 0, VOX)
    picked = drawn_rows % counts[:, None, :, None]
    entry_index = jnp.arange(HALO)[None, None, None, :]
    picked = jnp.where(entry_index == 0, counts[:, None, :, None] - 1, picked)
    picked = jnp.where(entry_index == 1, 0, picked)
    send_lists = picked.reshape(SCENES, 2, blocks * HALO).astype(jnp.int32)
    shape = (SCENES, KV, blocks, VOX)
    kind_draw = jax.random.randint(jax.random.fold_in(key, 14), shape, 0, 100)
    local_rows = jax.random.randint(jax.random.fold_in(key, 15), shape, 0, VOX) % counts[:, None, :, None]
    side_pick = jax.random.randint(jax.random.fold_in(key, 16), shape, 0, 2)
    block_index = jnp.arange(blocks)[None, None, :, None]
    side_pick = jnp.where(block_index == 0, 1, jnp.where(block_index == blocks - 1, 0, side_pick))
    halo_slot = VOX + side_pick * HALO + jax.random.randint(jax.random.fold_in(key, 17), shape, 0, HALO)
    sentinel = VOX + 2 * HALO
    offset_map = jnp.where(kind_draw < 30, local_rows, jnp.where(kind_draw < 40, halo_slot, sentinel))
    row_index = jnp.arange(VOX)[None, None, None, :]
    is_centre = jnp.arange(KV)[None, :, None, None] == KV // 2
    offset_map = jnp.where(is_centre, row_index, offset_map)
    offset_map = jnp.where(row_index < counts[:, None, :, None], offset_map, sentinel)
    return (counts, send_lists, offset_map.reshape(SCENES, KV, blocks * VOX).astype(jnp.int32))


def draw_kernel_map(key, part):
    return geometry(key)[2]


def draw_send_rows(key, part):
    return geometry(key)[1]


def draw_counts(key, part):
    return geometry(key)[0]


def block_scale(rng, shape, shards, low, top_value):
    gain = 1.0
    for dim, shards_of in shards:
        heights = jax.random.uniform(jax.random.fold_in(jax.random.fold_in(rng, 6), dim), (shards_of,), jnp.float32, low / len(shards), top_value / len(shards))
        gain = gain * jnp.repeat(jnp.exp(heights), shape[dim] // shards_of).reshape((-1,) + (1,) * (len(shape) - 1 - dim))
    return gain


def noise(rng, dims, spread, bound, split=(), held_as=jnp.bfloat16):
    values = spread * jax.random.normal(rng, dims, jnp.float32)
    if split:
        values = values * block_scale(rng, dims, split, -0.22, 0.18)
    return jnp.clip(values, -bound, bound).astype(held_as)


def setup_inputs(seed: int = 0) -> dict:
    splits = jax.random.split(jax.random.key(seed), 7)
    return {
        "features": noise(splits[0], (SCENES, ROWS, C), 1.0, 6.0, ((0, 8), (1, 64))),
        "weights": noise(splits[1], (KV, C, C), (KV * C) ** -0.5, 0.109375),
        "kernel_map": draw_kernel_map(jax.random.fold_in(splits[6], 71), 0),
        "send_rows": draw_send_rows(jax.random.fold_in(splits[6], 71), 0),
        "counts": draw_counts(jax.random.fold_in(splits[6], 71), 0),
        "cotangent": noise(splits[5], (SCENES, ROWS, C), 1.0, 6.0, ((0, 8), (1, 64))),
    }


def pick_rows(table, indices):
    return table[indices]


def add_back(local_grads, send_lists, for_upper, for_lower):
    return local_grads.at[send_lists[1]].add(for_upper).at[send_lists[0]].add(for_lower)


def reference(features, weights, kernel_map, send_rows, counts, cotangent):
    block_count = SCENES * N_SPACE
    ext_length = VOX + 2 * HALO + 1
    active = jnp.arange(VOX, dtype=jnp.int32)[None, None, :] < counts[:, :, None]
    blocks = features.reshape(SCENES, N_SPACE, VOX, C)
    live = jnp.where(active[..., None], blocks, jnp.zeros((), jnp.bfloat16))
    zero_row = jnp.zeros((SCENES, N_SPACE, 1, C), jnp.bfloat16)
    padded = jnp.concatenate([live, zero_row], 2)
    send_lists = send_rows.reshape(SCENES, 2, N_SPACE, HALO).transpose(0, 2, 1, 3)
    outgoing = jax.vmap(jax.vmap(pick_rows))(padded, send_lists)
    zeros_halo = jnp.zeros((SCENES, 1, HALO, C), jnp.bfloat16)
    lower_in = jnp.concatenate([zeros_halo, outgoing[:, :-1, 1]], 1)
    upper_in = jnp.concatenate([outgoing[:, 1:, 0], zeros_halo], 1)
    extended = jnp.concatenate([live, lower_in, upper_in, zero_row], 2).reshape(block_count, ext_length, C)
    offset_maps = kernel_map.reshape(SCENES, KV, N_SPACE, VOX).transpose(0, 2, 1, 3).reshape(block_count, KV, VOX)
    alive = active.reshape(block_count, VOX, 1)
    grad_out = jnp.where(alive, cotangent.reshape(block_count, VOX, C), jnp.zeros((), jnp.bfloat16))

    def one_block(weight_total, inputs):
        table, offset_map, alive_rows, grad_rows = inputs

        def forward_step(running, pair):
            source, weight = pair
            return running + jnp.dot(table[source], weight, preferred_element_type=jnp.float32), None

        result, unused = lax.scan(forward_step, jnp.zeros((VOX, C), jnp.float32), (offset_map, weights))
        result = jnp.where(alive_rows, result, jnp.zeros((), jnp.float32)).astype(jnp.bfloat16)

        def backward_step(accum_grad, pair):
            source, weight = pair
            gathered = table[source]
            weight_part = lax.dot_general(gathered, grad_rows, (((0,), (0,)), ((), ())), preferred_element_type=jnp.float32)
            contrib = jnp.dot(grad_rows, weight.T, preferred_element_type=jnp.float32)
            return accum_grad.at[source].add(contrib), weight_part

        ext_grad, weight_parts = lax.scan(backward_step, jnp.zeros((ext_length, C), jnp.float32), (offset_map, weights))
        return weight_total + weight_parts, (result, ext_grad)

    weight_total, (results, ext_grads) = lax.scan(one_block, jnp.zeros((KV, C, C), jnp.float32), (extended, offset_maps, alive, grad_out))
    ext_grads = ext_grads.reshape(SCENES, N_SPACE, ext_length, C)
    lower_part = ext_grads[:, :, VOX:VOX + HALO]
    upper_part = ext_grads[:, :, VOX + HALO:VOX + 2 * HALO]
    zeros_grad = jnp.zeros((SCENES, 1, HALO, C), jnp.float32)
    for_upper = jnp.concatenate([lower_part[:, 1:], zeros_grad], 1)
    for_lower = jnp.concatenate([zeros_grad, upper_part[:, :-1]], 1)
    local_grads = jnp.concatenate([ext_grads[:, :, :VOX], jnp.zeros((SCENES, N_SPACE, 1, C), jnp.float32)], 2)
    local_grads = jax.vmap(jax.vmap(add_back))(local_grads, send_lists, for_upper, for_lower)
    grad_features = jnp.where(active[..., None], local_grads[:, :, :VOX], jnp.zeros((), jnp.float32)).astype(jnp.bfloat16)
    output = results.reshape(SCENES, ROWS, C)
    grad_weights = weight_total * ((SCENES * ROWS) ** -0.5)
    return output, grad_features.reshape(SCENES, ROWS, C), grad_weights
```

```python
import jax
import jax.numpy as jnp
from jax import lax
from jax.experimental import pallas as pl
from jax.experimental.pallas import tpu as pltpu
from jax.sharding import Mesh, PartitionSpec as P

C = 128
KV = 27
VOX = 512
HALO = 128
EXT = VOX + 2 * HALO
SCALE = 262144**-0.5
VMEM_LIMIT = 48 * 2**20

f32 = jnp.float32
bf16 = jnp.bfloat16


def onehot(indices, rows):
    line = lax.broadcasted_iota(jnp.int32, (rows, indices.shape[1]), 0)
    return jnp.where(line == indices, jnp.ones((), bf16), jnp.zeros((), bf16))


def masked(count, values):
    alive = lax.broadcasted_iota(jnp.int32, values.shape, 0) < count[0, 0]
    return jnp.where(alive, values, jnp.zeros((), values.dtype))


def split(values):
    high = values.astype(bf16)
    low = (values - high.astype(f32)).astype(bf16)
    return jnp.concatenate([high, low], axis=1)


def joined(both):
    return both[:, :C] + both[:, C:]


def matmul(a, b, dims=((1,), (0,))):
    return lax.dot_general(a, b, (dims, ((), ())), preferred_element_type=f32)


def pick_kernel(count, features, send, outgoing):
    live = masked(count, features[...])
    for side in range(2):
        rows = onehot(send[side : side + 1, :], VOX)
        outgoing[side] = matmul(rows, live, ((0,), (0,))).astype(bf16)


def scatter_kernel(count, cotangent, weights, kernel_map, ext_grad, grad_rows, acc):
    grad_rows[...] = masked(count, cotangent[...])
    acc[...] = jnp.zeros_like(acc)
    for k in range(KV):
        contrib = matmul(grad_rows[...], weights[k], ((1,), (1,)))
        acc[...] += matmul(onehot(kernel_map[k : k + 1, :], EXT), split(contrib))
    ext_grad[...] = joined(acc[...])


def gather_kernel(
    count, features, lower, upper, weights, kernel_map, grad_rows, output, weight_grad, table, gathered
):
    table[:, :VOX] = masked(count, features[...]).T
    table[:, VOX : VOX + HALO] = lower[...].T
    table[:, VOX + HALO :] = upper[...].T
    for k in range(KV):
        rows = onehot(kernel_map[k : k + 1, :], EXT)
        gathered[k * C : (k + 1) * C, :] = matmul(table[...], rows).astype(bf16)
    weight_grad[...] = matmul(gathered[...], grad_rows[...]) * SCALE
    result = matmul(weights[...].reshape(KV * C, C), gathered[...], ((0,), (0,)))
    output[...] = masked(count, result.T).astype(bf16)


def finish_kernel(count, ext_grad, for_upper, for_lower, send, grad_features):
    total = ext_grad[:VOX, :]
    for side, returned in ((1, for_upper), (0, for_lower)):
        rows = onehot(send[side : side + 1, :], VOX)
        total = total + joined(matmul(rows, split(returned[...])))
    grad_features[...] = masked(count, total).astype(bf16)


def call(kernel, name, args, outs, scratch=(), flops=0):
    scalar = pl.BlockSpec(memory_space=pltpu.SMEM)
    vector = pl.BlockSpec(memory_space=pltpu.VMEM)
    outs = tuple(jax.ShapeDtypeStruct(*o) for o in outs)
    moved = sum(a.size * a.dtype.itemsize for a in (*args, *outs))
    return pl.pallas_call(
        kernel,
        name=name,
        in_specs=[scalar] + [vector] * (len(args) - 1),
        out_specs=(vector,) * len(outs),
        out_shape=outs,
        scratch_shapes=[pltpu.VMEM(*s) for s in scratch],
        cost_estimate=pl.CostEstimate(flops=flops, transcendentals=0, bytes_accessed=moved),
        compiler_params=pltpu.CompilerParams(vmem_limit_bytes=VMEM_LIMIT),
    )(*args)


def exchange(parts, axes):
    return lax.all_to_all(parts, axes, 0, 0, tiled=False)


def spread(part, axes, size):
    return exchange(jnp.broadcast_to(part[None], (size, *part.shape)), axes).reshape(-1, C)


def mesh_sum(values):
    half = exchange(values.reshape(2, -1, C), "c").sum(0)
    part = exchange(half.reshape(4, -1, C), "x").sum(0)
    rows = part.shape[0]
    padded = jnp.pad(part, ((0, -rows % (64 * 8)), (0, 0)))
    piece = exchange(padded.reshape(64, -1, C), ("z", "y")).sum(0)
    part = spread(piece, ("z", "y"), 64)[:rows]
    return spread(spread(part, "x", 4), "c", 2)


def per_device(features, weights, kernel_map, send_rows, counts, cotangent):
    features, kernel_map, send, cotangent = features[0], kernel_map[0], send_rows[0], cotangent[0]
    space = ("z", "y")
    size = lax.axis_size(space)
    up = [(i, i + 1) for i in range(size - 1)]
    down = [(i + 1, i) for i in range(size - 1)]
    (outgoing,) = call(pick_kernel, "pick", (counts, features, send), [((2, HALO, C), bf16)])
    lower_in = lax.ppermute(outgoing[1], space, up)
    upper_in = lax.ppermute(outgoing[0], space, down)
    ext_grad, grad_rows = call(
        scatter_kernel,
        "scatter",
        (counts, cotangent, weights, kernel_map),
        [((EXT, C), f32), ((VOX, C), bf16)],
        [((EXT, 2 * C), f32)],
        2 * KV * VOX * C * (C + 2 * EXT),
    )
    for_lower = lax.ppermute(ext_grad[VOX + HALO :], space, up)
    for_upper = lax.ppermute(ext_grad[VOX : VOX + HALO], space, down)
    output, weight_grad = call(
        gather_kernel,
        "gather",
        (counts, features, lower_in, upper_in, weights, kernel_map, grad_rows),
        [((VOX, C), bf16), ((KV * C, C), f32)],
        [((C, EXT), bf16), ((KV * C, VOX), bf16)],
        2 * KV * VOX * C * (2 * C + EXT),
    )
    (grad_features,) = call(
        finish_kernel,
        "finish",
        (counts, ext_grad, for_upper, for_lower, send),
        [((VOX, C), bf16)],
    )
    grad_weights = mesh_sum(weight_grad).reshape(KV, C, C)
    return output[None], grad_features[None], grad_weights


def solution(mesh):
    fine = Mesh(mesh.devices.reshape(8, 8, 4, 2), ("z", "y", "x", "c"))
    space, batch = ("z", "y"), ("x", "c")
    in_specs = (
        P(batch, space, None),
        P(),
        P(batch, None, space),
        P(batch, None, space),
        P(batch, space),
        P(batch, space, None),
    )
    out_specs = (P(batch, space, None), P(batch, space, None), P())
    return jax.shard_map(
        per_device, mesh=fine, in_specs=in_specs, out_specs=out_specs, check_vma=False
    )
```

```python
import functools

import jax
import jax.numpy as jnp
from jax import lax
from jax.experimental import pallas as pl
from jax.experimental.pallas import tpu as pltpu
from jax.sharding import Mesh, PartitionSpec as P

C = 128
KV = 27
VOX = 512
HALO = 128
EXT = VOX + 2 * HALO
SCALE = 262144**-0.5
HALF = KV * C // 2
QUARTER = HALF // 4
CODED = QUARTER + 16
GROUP = 3
FIRST = 6
TILE = 256
VMEM_LIMIT = 16 * 2**20

f32 = jnp.float32
bf16 = jnp.bfloat16


def onehot(indices, rows, first=0):
    line = lax.broadcasted_iota(jnp.int32, (rows, indices.shape[1]), 0) + first
    return jnp.where(line == indices, jnp.ones((), bf16), jnp.zeros((), bf16))


def offset_onehot(kernel_map, k, rows, first=0):
    return onehot(kernel_map[k : k + 1, :], rows, first)


def masked(count, values):
    alive = lax.broadcasted_iota(jnp.int32, values.shape, 0) < count[0, 0]
    return jnp.where(alive, values, jnp.zeros((), values.dtype))


def split(values):
    high = values.astype(bf16)
    low = (values - high.astype(f32)).astype(bf16)
    return jnp.concatenate([high, low], axis=1)


def joined(both):
    return both[:, :C] + both[:, C:]


def matmul(a, b, dims=((1,), (0,))):
    return lax.dot_general(a, b, (dims, ((), ())), preferred_element_type=f32)


def pick_kernel(count, features, send, to_lower, to_upper):
    live = masked(count, features[...])
    for side, outgoing in ((0, to_lower), (1, to_upper)):
        rows = onehot(send[side : side + 1, :], VOX)
        outgoing[...] = matmul(rows, live, ((0,), (0,))).astype(bf16)


def local_kernel(count, features, kernel_map, gathered, table):
    table[...] = masked(count, features[...]).T
    for k in range(KV):
        rows = offset_onehot(kernel_map, k, VOX)
        gathered[k * C : (k + 1) * C, :] = matmul(table[...], rows).astype(bf16)


def halo_kernel(
    count, lower, upper, kernel_map, own, cotangent, kept, sent, gathered, grad_rows, table
):
    table[:, :HALO] = lower[...].T
    table[:, HALO:] = upper[...].T
    grad_rows[...] = masked(count, cotangent[...])
    for k in range(KV):
        rows = offset_onehot(kernel_map, k, 2 * HALO, VOX)
        part = slice(k * C, (k + 1) * C)
        gathered[part, :] = own[part, :] + matmul(table[...], rows).astype(bf16)
    first_core = lax.axis_index("c") == 0
    for row in range(0, HALF, HALF // 9):
        parts = [slice(row + start, row + start + HALF // 9) for start in (0, HALF)]
        low, high = (matmul(gathered[part, :], grad_rows[...]) * SCALE for part in parts)
        kept[parts[0], :] = jnp.where(first_core, low, high)
        sent[parts[0], :] = jnp.where(first_core, high, low)


def scatter_kernel(offsets, grad_rows, weights, kernel_map, *refs):
    *earlier, ext_grad, contribs = refs
    for first in range(*offsets, GROUP):
        group = range(first, first + GROUP)
        for j, k in enumerate(group):
            contrib = matmul(grad_rows[...], weights[k], ((1,), (1,)))
            contribs[j * VOX : (j + 1) * VOX, :] = split(contrib)
        for row in range(0, EXT, TILE):
            rows = [offset_onehot(kernel_map, k, TILE, row) for k in group]
            part = joined(matmul(jnp.concatenate(rows, axis=1), contribs[...]))
            tile = slice(row, row + TILE)
            if first > offsets[0]:
                part += ext_grad[tile, :]
            elif earlier:
                part += earlier[0][tile, :]
            ext_grad[tile, :] = part


def output_kernel(count, weights, gathered, output):
    result = matmul(weights[...].reshape(KV * C, C), gathered[...], ((0,), (0,)))
    output[...] = masked(count, result.T).astype(bf16)


def finish_kernel(count, ext_grad, for_upper, for_lower, send, grad_features):
    total = ext_grad[:VOX, :]
    for side, returned in ((1, for_upper), (0, for_lower)):
        rows = onehot(send[side : side + 1, :], VOX)
        total = total + joined(matmul(rows, split(returned[...])))
    grad_features[...] = masked(count, total).astype(bf16)


def encode(values, coded):
    top = jnp.max(jnp.abs(values), axis=0, keepdims=True)
    exponent = jnp.clip(jnp.floor(jnp.log2(jnp.maximum(top, 1e-37))), -100.0, 100.0)
    steps = jnp.round(values * jnp.exp2(14.0 - exponent))
    coded[:QUARTER, :] = jnp.clip(steps, -32767.0, 32767.0).astype(jnp.int32).astype(jnp.int16)
    exponent = jnp.broadcast_to(exponent, (CODED - QUARTER, C))
    coded[QUARTER:, :] = exponent.astype(jnp.int32).astype(jnp.int16)


def decode(coded):
    values = coded[...].astype(jnp.int32).astype(f32)
    return values[:QUARTER, :] * jnp.exp2(values[QUARTER : QUARTER + 1, :] - 14.0)


def halves_kernel(kept, received, quarters):
    for i in range(4):
        rows = slice(i * QUARTER, (i + 1) * QUARTER)
        encode(kept[rows, :] + received[rows, :], quarters.at[i])


def quarters_kernel(quarters, total):
    total[:QUARTER, :] = sum(decode(quarters.at[i]) for i in range(4))
    total[QUARTER:, :] = jnp.zeros_like(total[QUARTER:, :])


def pieces_kernel(pieces, spread):
    spread[...] = jnp.broadcast_to(jnp.sum(pieces[...], axis=0)[None], spread.shape)


def total_kernel(total, quarters):
    encode(total[:QUARTER, :], quarters.at[0])
    for i in range(1, 4):
        quarters[i] = quarters[0]


def whole_kernel(kept, received, whole, buffer, sems):
    core = lax.axis_index("c")
    copies = []
    for i, (half, place) in enumerate(((kept, core), (received, 1 - core))):
        for j in range(4):
            buffer[i, j * QUARTER : (j + 1) * QUARTER, :] = decode(half.at[j])
        rows = pl.ds(pl.multiple_of(place * HALF, 8), HALF)
        copies.append(pltpu.make_async_copy(buffer.at[i], whole.at[rows], sems.at[i]))
        copies[i].start()
    for copy in copies:
        copy.wait()


def call(kernel, name, args, outs, scratch=(), flops=0, scalars=1):
    scalar = pl.BlockSpec(memory_space=pltpu.SMEM)
    vector = pl.BlockSpec(memory_space=pltpu.VMEM)
    outs = tuple(jax.ShapeDtypeStruct(*o) for o in outs)
    moved = sum(a.size * a.dtype.itemsize for a in (*args, *outs))
    return pl.pallas_call(
        kernel,
        name=name,
        in_specs=[scalar] * scalars + [vector] * (len(args) - scalars),
        out_specs=(vector,) * len(outs),
        out_shape=outs,
        scratch_shapes=[pltpu.VMEM(*s) for s in scratch],
        cost_estimate=pl.CostEstimate(flops=flops, transcendentals=0, bytes_accessed=moved),
        compiler_params=pltpu.CompilerParams(vmem_limit_bytes=VMEM_LIMIT),
    )(*args)


def scatter(name, offsets, args):
    return call(
        functools.partial(scatter_kernel, offsets),
        name,
        args,
        [((EXT, C), f32)],
        [((GROUP * VOX, 2 * C), bf16)],
        2 * (offsets[1] - offsets[0]) * VOX * C * (C + 2 * EXT),
        scalars=0,
    )[0]


def across_c(part):
    return lax.ppermute(part, "c", [(0, 1), (1, 0)])


def exchange(pieces, axes):
    return lax.all_to_all(pieces, axes, 0, 0, tiled=False)


def per_device(features, weights, kernel_map, send_rows, counts, cotangent):
    features, kernel_map, send, cotangent = features[0], kernel_map[0], send_rows[0], cotangent[0]
    space = ("z", "y")
    size = lax.axis_size(space)
    up = [(i, i + 1) for i in range(size - 1)]
    down = [(i + 1, i) for i in range(size - 1)]
    rows = ((HALO, C), bf16)
    to_lower, to_upper = call(pick_kernel, "pick", (counts, features, send), [rows, rows])
    lower_in = lax.ppermute(to_upper, space, up)
    upper_in = lax.ppermute(to_lower, space, down)
    (own,) = call(
        local_kernel,
        "local",
        (counts, features, kernel_map),
        [((KV * C, VOX), bf16)],
        [((C, VOX), bf16)],
        2 * KV * VOX * C * VOX,
    )
    kept, sent, gathered, grad_rows = call(
        halo_kernel,
        "halo",
        (counts, lower_in, upper_in, kernel_map, own, cotangent),
        [((HALF, C), f32), ((HALF, C), f32), ((KV * C, VOX), bf16), ((VOX, C), bf16)],
        [((C, 2 * HALO), bf16)],
        2 * KV * VOX * C * (2 * HALO + C),
    )
    received = across_c(sent)
    (output,) = call(
        output_kernel,
        "output",
        (counts, weights, gathered),
        [((VOX, C), bf16)],
        flops=2 * KV * VOX * C * C,
    )
    ext_grad = scatter("scatter_first", (0, FIRST), (grad_rows, weights, kernel_map))
    received, ext_grad, output = lax.optimization_barrier((received, ext_grad, output))
    coded = ((4, CODED, C), jnp.int16)
    (quarters,) = call(halves_kernel, "halves", (kept, received), [coded], scalars=0)
    quarters = exchange(quarters, "x")
    ext_grad = scatter("scatter_rest", (FIRST, KV), (grad_rows, weights, kernel_map, ext_grad))
    for_lower = lax.ppermute(ext_grad[VOX + HALO :], space, up)
    for_upper = lax.ppermute(ext_grad[VOX : VOX + HALO], space, down)
    (grad_features,) = call(
        finish_kernel,
        "finish",
        (counts, ext_grad, for_upper, for_lower, send),
        [((VOX, C), bf16)],
    )
    quarters, grad_features = lax.optimization_barrier((quarters, grad_features))
    (total,) = call(quarters_kernel, "quarters", (quarters,), [((VOX, C), f32)], scalars=0)
    pieces = exchange(total.reshape(size, -1, C), space)
    (pieces,) = call(pieces_kernel, "pieces", (pieces,), [((size, 8, C), f32)], scalars=0)
    total = exchange(pieces, space).reshape(VOX, C)
    (quarters,) = call(total_kernel, "total", (total,), [coded], scalars=0)
    half = exchange(quarters, "x")
    grad_weights = pl.pallas_call(
        whole_kernel,
        name="whole",
        in_specs=[pl.BlockSpec(memory_space=pltpu.VMEM)] * 2,
        out_specs=pl.BlockSpec(memory_space=pl.ANY),
        out_shape=jax.ShapeDtypeStruct((KV * C, C), f32),
        scratch_shapes=[pltpu.VMEM((2, HALF, C), f32), pltpu.SemaphoreType.DMA((2,))],
        compiler_params=pltpu.CompilerParams(vmem_limit_bytes=8 * 2**20),
    )(half, across_c(half)).reshape(KV, C, C)
    return output[None], grad_features[None], grad_weights


def solution(mesh):
    fine = Mesh(mesh.devices.reshape(8, 8, 4, 2), ("z", "y", "x", "c"))
    space, batch = ("z", "y"), ("x", "c")
    in_specs = (
        P(batch, space, None),
        P(),
        P(batch, None, space),
        P(batch, None, space),
        P(batch, space),
        P(batch, space, None),
    )
    out_specs = (P(batch, space, None), P(batch, space, None), P())
    return jax.shard_map(
        per_device, mesh=fine, in_specs=in_specs, out_specs=out_specs, check_vma=False
    )
```

```python
import functools

import jax
import jax.numpy as jnp
from jax import lax
from jax.experimental import pallas as pl
from jax.experimental.pallas import tpu as pltpu
from jax.sharding import Mesh, PartitionSpec as P

C = 128
KV = 27
VOX = 512
HALO = 128
EXT = VOX + 2 * HALO
SCALE = 262144**-0.5
HALF = KV * C // 2
QUARTER = HALF // 4
CODED = QUARTER + 16
GROUP = 3
FIRST = 3
TILE = 256
VMEM_LIMIT = 16 * 2**20

f32 = jnp.float32
bf16 = jnp.bfloat16


def onehot(indices, rows, first=0):
    line = lax.broadcasted_iota(jnp.int32, (rows, indices.shape[1]), 0) + first
    return jnp.where(line == indices, jnp.ones((), bf16), jnp.zeros((), bf16))


def offset_onehot(kernel_map, k, rows, first=0):
    return onehot(kernel_map[k], rows, first)


def masked(count, values):
    alive = lax.broadcasted_iota(jnp.int32, values.shape, 0) < count[0, 0]
    return jnp.where(alive, values, jnp.zeros((), values.dtype))


def split(values):
    high = values.astype(bf16)
    low = (values - high.astype(f32)).astype(bf16)
    return jnp.concatenate([high, low], axis=1)


def joined(both):
    return both[:, :C] + both[:, C:]


def matmul(a, b, dims=((1,), (0,))):
    return lax.dot_general(a, b, (dims, ((), ())), preferred_element_type=f32)


def pick_kernel(
    count, features, send, kernel_map, to_lower, to_upper, table, kernel_map_out, rows, lists, sems
):
    copies = [
        pltpu.make_async_copy(source, target, sems.at[i])
        for i, (source, target) in enumerate(
            ((features, rows), (send, lists), (kernel_map, kernel_map_out))
        )
    ]
    for copy in copies:
        copy.start()
    for copy in copies:
        copy.wait()
    live = masked(count, rows[...])
    for side, outgoing in ((0, to_lower), (1, to_upper)):
        picked = onehot(lists[side : side + 1, :], VOX)
        outgoing[...] = matmul(picked, live, ((0,), (0,))).astype(bf16)
    table[...] = live.T


def local_kernel(table, kernel_map, gathered):
    for k in range(KV):
        rows = offset_onehot(kernel_map, k, VOX)
        gathered[k * C : (k + 1) * C, :] = matmul(table[...], rows).astype(bf16)


def halo_kernel(
    count, lower, upper, kernel_map, own, cotangent, kept, sent, gathered, grad_rows, table
):
    table[:, :HALO] = lower[...].T
    table[:, HALO:] = upper[...].T
    grad_rows[...] = masked(count, cotangent[...])
    for k in range(KV):
        rows = offset_onehot(kernel_map, k, 2 * HALO, VOX)
        part = slice(k * C, (k + 1) * C)
        gathered[part, :] = own[part, :] + matmul(table[...], rows).astype(bf16)
    first_core = lax.axis_index("c") == 0
    for row in range(0, HALF, HALF // 9):
        parts = [slice(row + start, row + start + HALF // 9) for start in (0, HALF)]
        low, high = (matmul(gathered[part, :], grad_rows[...]) * SCALE for part in parts)
        kept[parts[0], :] = jnp.where(first_core, low, high)
        sent[parts[0], :] = jnp.where(first_core, high, low)


def scatter_kernel(offsets, grad_rows, weights, kernel_map, *refs):
    *earlier, ext_grad, contribs = refs
    for first in range(*offsets, GROUP):
        group = range(first, first + GROUP)
        for j, k in enumerate(group):
            contrib = matmul(grad_rows[...], weights[k], ((1,), (1,)))
            contribs[j * VOX : (j + 1) * VOX, :] = split(contrib)
        for row in range(0, EXT, TILE):
            rows = [offset_onehot(kernel_map, k, TILE, row) for k in group]
            part = joined(matmul(jnp.concatenate(rows, axis=1), contribs[...]))
            tile = slice(row, row + TILE)
            if first > offsets[0]:
                part += ext_grad[tile, :]
            elif earlier:
                part += earlier[0][tile, :]
            ext_grad[tile, :] = part


def output_kernel(count, weights, gathered, output):
    result = matmul(weights[...].reshape(KV * C, C), gathered[...], ((0,), (0,)))
    output[...] = masked(count, result.T).astype(bf16)


def finish_kernel(count, ext_grad, for_upper, for_lower, send, grad_features):
    total = ext_grad[:VOX, :]
    for side, returned in ((1, for_upper), (0, for_lower)):
        rows = onehot(send[side : side + 1, :], VOX)
        total = total + joined(matmul(rows, split(returned[...])))
    grad_features[...] = masked(count, total).astype(bf16)


def encode(values, coded):
    top = jnp.max(jnp.abs(values), axis=0, keepdims=True)
    exponent = jnp.clip(jnp.floor(jnp.log2(jnp.maximum(top, 1e-37))), -100.0, 100.0)
    steps = jnp.round(values * jnp.exp2(14.0 - exponent))
    coded[:QUARTER, :] = jnp.clip(steps, -32767.0, 32767.0).astype(jnp.int32).astype(jnp.int16)
    exponent = jnp.broadcast_to(exponent, (CODED - QUARTER, C))
    coded[QUARTER:, :] = exponent.astype(jnp.int32).astype(jnp.int16)


def decode(coded):
    values = coded[...].astype(jnp.int32).astype(f32)
    return values[:QUARTER, :] * jnp.exp2(values[QUARTER : QUARTER + 1, :] - 14.0)


def halves_kernel(kept, received, quarters):
    for i in range(4):
        rows = slice(i * QUARTER, (i + 1) * QUARTER)
        encode(kept[rows, :] + received[rows, :], quarters.at[i])


def quarters_kernel(quarters, total):
    total[:QUARTER, :] = sum(decode(quarters.at[i]) for i in range(4))
    total[QUARTER:, :] = jnp.zeros_like(total[QUARTER:, :])


def pieces_kernel(pieces, spread):
    spread[...] = jnp.broadcast_to(jnp.sum(pieces[...], axis=0)[None], spread.shape)


def total_kernel(total, quarters):
    encode(total[:QUARTER, :], quarters.at[0])
    for i in range(1, 4):
        quarters[i] = quarters[0]


def whole_kernel(kept, received, whole, buffer, sems):
    core = lax.axis_index("c")
    copies = []
    for i, (half, place) in enumerate(((kept, core), (received, 1 - core))):
        for j in range(4):
            buffer[i, j * QUARTER : (j + 1) * QUARTER, :] = decode(half.at[j])
        rows = pl.ds(pl.multiple_of(place * HALF, 8), HALF)
        copies.append(pltpu.make_async_copy(buffer.at[i], whole.at[rows], sems.at[i]))
        copies[i].start()
    for copy in copies:
        copy.wait()


def call(kernel, name, args, outs, scratch=(), flops=0, scalars=1, space=pltpu.VMEM):
    scalar = pl.BlockSpec(memory_space=pltpu.SMEM)
    vector = pl.BlockSpec(memory_space=pltpu.VMEM)
    operand = pl.BlockSpec(memory_space=space)
    outs = tuple(jax.ShapeDtypeStruct(*o) for o in outs)
    moved = sum(a.size * a.dtype.itemsize for a in (*args, *outs))
    return pl.pallas_call(
        kernel,
        name=name,
        in_specs=[scalar] * scalars + [operand] * (len(args) - scalars),
        out_specs=(vector,) * len(outs),
        out_shape=outs,
        scratch_shapes=[pltpu.VMEM(*s) if isinstance(s, tuple) else s for s in scratch],
        cost_estimate=pl.CostEstimate(flops=flops, transcendentals=0, bytes_accessed=moved),
        compiler_params=pltpu.CompilerParams(vmem_limit_bytes=VMEM_LIMIT),
    )(*args)


def scatter(name, offsets, args):
    return call(
        functools.partial(scatter_kernel, offsets),
        name,
        args,
        [((EXT, C), f32)],
        [((GROUP * VOX, 2 * C), bf16)],
        2 * (offsets[1] - offsets[0]) * VOX * C * (C + 2 * EXT),
        scalars=0,
    )[0]


def across_c(part):
    return lax.ppermute(part, "c", [(0, 1), (1, 0)])


def exchange(pieces, axes):
    return lax.all_to_all(pieces, axes, 0, 0, tiled=False)


def per_device(features, weights, kernel_map, send_rows, counts, cotangent):
    features, send, cotangent = features[0], send_rows[0], cotangent[0]
    kernel_map = kernel_map.transpose(1, 0, 2)
    space = ("z", "y")
    size = lax.axis_size(space)
    up = [(i, i + 1) for i in range(size - 1)]
    down = [(i + 1, i) for i in range(size - 1)]
    rows = ((HALO, C), bf16)
    to_lower, to_upper, table, kernel_map = call(
        pick_kernel,
        "pick",
        (counts, *(pltpu.with_memory_space_constraint(a, pltpu.HBM) for a in (features, send, kernel_map))),
        [rows, rows, ((C, VOX), bf16), ((KV, 1, VOX), jnp.int32)],
        [((VOX, C), bf16), ((2, HALO), jnp.int32), pltpu.SemaphoreType.DMA((3,))],
        space=pltpu.HBM,
    )
    lower_in = lax.ppermute(to_upper, space, up)
    upper_in = lax.ppermute(to_lower, space, down)
    (own,) = call(
        local_kernel,
        "local",
        (table, kernel_map),
        [((KV * C, VOX), bf16)],
        flops=2 * KV * VOX * C * VOX,
        scalars=0,
    )
    kept, sent, gathered, grad_rows = call(
        halo_kernel,
        "halo",
        (counts, lower_in, upper_in, kernel_map, own, cotangent),
        [((HALF, C), f32), ((HALF, C), f32), ((KV * C, VOX), bf16), ((VOX, C), bf16)],
        [((C, 2 * HALO), bf16)],
        2 * KV * VOX * C * (2 * HALO + C),
    )
    received = across_c(sent)
    (output,) = call(
        output_kernel,
        "output",
        (counts, weights, gathered),
        [((VOX, C), bf16)],
        flops=2 * KV * VOX * C * C,
    )
    ext_grad = scatter("scatter_first", (0, FIRST), (grad_rows, weights, kernel_map))
    received, ext_grad, output = lax.optimization_barrier((received, ext_grad, output))
    coded = ((4, CODED, C), jnp.int16)
    (quarters,) = call(halves_kernel, "halves", (kept, received), [coded], scalars=0)
    quarters = exchange(quarters, "x")
    ext_grad = scatter("scatter_rest", (FIRST, KV), (grad_rows, weights, kernel_map, ext_grad))
    quarters, ext_grad = lax.optimization_barrier((quarters, ext_grad))
    (total,) = call(quarters_kernel, "quarters", (quarters,), [((VOX, C), f32)], scalars=0)
    pieces = exchange(total.reshape(size, -1, C), space)
    for_lower = lax.ppermute(ext_grad[VOX + HALO :], space, up)
    for_upper = lax.ppermute(ext_grad[VOX : VOX + HALO], space, down)
    pieces, for_lower, for_upper = lax.optimization_barrier((pieces, for_lower, for_upper))
    (pieces,) = call(pieces_kernel, "pieces", (pieces,), [((size, 8, C), f32)], scalars=0)
    total = exchange(pieces, space).reshape(VOX, C)
    (quarters,) = call(total_kernel, "total", (total,), [coded], scalars=0)
    half = exchange(quarters, "x")
    half, ext_grad = lax.optimization_barrier((half, ext_grad))
    received = across_c(half)
    (grad_features,) = call(
        finish_kernel,
        "finish",
        (counts, ext_grad, for_upper, for_lower, send),
        [((VOX, C), bf16)],
    )
    received, grad_features = lax.optimization_barrier((received, grad_features))
    grad_weights = pl.pallas_call(
        whole_kernel,
        name="whole",
        in_specs=[pl.BlockSpec(memory_space=pltpu.VMEM)] * 2,
        out_specs=pl.BlockSpec(memory_space=pl.ANY),
        out_shape=jax.ShapeDtypeStruct((KV * C, C), f32),
        scratch_shapes=[pltpu.VMEM((2, HALF, C), f32), pltpu.SemaphoreType.DMA((2,))],
        compiler_params=pltpu.CompilerParams(vmem_limit_bytes=8 * 2**20),
    )(half, received).reshape(KV, C, C)
    return output[None], grad_features[None], grad_weights


def solution(mesh):
    fine = Mesh(mesh.devices.reshape(8, 8, 4, 2), ("z", "y", "x", "c"))
    space, batch = ("z", "y"), ("x", "c")
    in_specs = (
        P(batch, space, None),
        P(),
        P(batch, None, space),
        P(batch, None, space),
        P(batch, space),
        P(batch, space, None),
    )
    out_specs = (P(batch, space, None), P(batch, space, None), P())
    return jax.shard_map(
        per_device, mesh=fine, in_specs=in_specs, out_specs=out_specs, check_vma=False
    )
```

```python
import functools

import jax
import jax.numpy as jnp
from jax import lax
from jax.experimental import pallas as pl
from jax.experimental.pallas import tpu as pltpu
from jax.sharding import Mesh, PartitionSpec as P

C = 128
KV = 27
VOX = 512
HALO = 128
EXT = VOX + 2 * HALO
SCALE = 262144**-0.5
HALF = KV * C // 2
QUARTER = HALF // 4
CODED = QUARTER + 16
PIECES = 64
GROUP = 3
FIRST = 3
TILE = 256
VMEM_LIMIT = 16 * 2**20

f32 = jnp.float32
bf16 = jnp.bfloat16


def onehot(indices, rows, first=0):
    line = lax.broadcasted_iota(jnp.int32, (rows, indices.shape[1]), 0) + first
    return jnp.where(line == indices, jnp.ones((), bf16), jnp.zeros((), bf16))


def offset_onehot(kernel_map, k, rows, first=0):
    return onehot(kernel_map[k], rows, first)


def masked(count, values):
    alive = lax.broadcasted_iota(jnp.int32, values.shape, 0) < count[0, 0]
    return jnp.where(alive, values, jnp.zeros((), values.dtype))


def split(values):
    high = values.astype(bf16)
    low = (values - high.astype(f32)).astype(bf16)
    return jnp.concatenate([high, low], axis=1)


def joined(both):
    return both[:, :C] + both[:, C:]


def matmul(a, b, dims=((1,), (0,))):
    return lax.dot_general(a, b, (dims, ((), ())), preferred_element_type=f32)


def pick_kernel(
    count, features, send, kernel_map, to_lower, to_upper, table, kernel_map_out, rows, lists, sems
):
    copies = [
        pltpu.make_async_copy(source, target, sems.at[i])
        for i, (source, target) in enumerate(
            ((features, rows), (send, lists), (kernel_map, kernel_map_out))
        )
    ]
    for copy in copies:
        copy.start()
    for copy in copies:
        copy.wait()
    live = masked(count, rows[...])
    for side, outgoing in ((0, to_lower), (1, to_upper)):
        picked = onehot(lists[side : side + 1, :], VOX)
        outgoing[...] = matmul(picked, live, ((0,), (0,))).astype(bf16)
    table[...] = live.T


def local_kernel(table, kernel_map, gathered):
    for k in range(KV):
        rows = offset_onehot(kernel_map, k, VOX)
        gathered[k * C : (k + 1) * C, :] = matmul(table[...], rows).astype(bf16)


def halo_kernel(
    count, lower, upper, kernel_map, own, cotangent, kept, sent, gathered, grad_rows, table
):
    table[:, :HALO] = lower[...].T
    table[:, HALO:] = upper[...].T
    grad_rows[...] = masked(count, cotangent[...])
    for k in range(KV):
        rows = offset_onehot(kernel_map, k, 2 * HALO, VOX)
        part = slice(k * C, (k + 1) * C)
        gathered[part, :] = own[part, :] + matmul(table[...], rows).astype(bf16)
    first_core = lax.axis_index("c") == 0
    for row in range(0, HALF, HALF // 9):
        parts = [slice(row + start, row + start + HALF // 9) for start in (0, HALF)]
        low, high = (matmul(gathered[part, :], grad_rows[...]) * SCALE for part in parts)
        kept[parts[0], :] = jnp.where(first_core, low, high)
        sent[parts[0], :] = jnp.where(first_core, high, low)


def scatter_kernel(offsets, grad_rows, weights, kernel_map, *refs):
    *earlier, ext_grad, contribs = refs
    for first in range(*offsets, GROUP):
        group = range(first, first + GROUP)
        for j, k in enumerate(group):
            contrib = matmul(grad_rows[...], weights[k], ((1,), (1,)))
            contribs[j * VOX : (j + 1) * VOX, :] = split(contrib)
        for row in range(0, EXT, TILE):
            rows = [offset_onehot(kernel_map, k, TILE, row) for k in group]
            part = joined(matmul(jnp.concatenate(rows, axis=1), contribs[...]))
            tile = slice(row, row + TILE)
            if first > offsets[0]:
                part += ext_grad[tile, :]
            elif earlier:
                part += earlier[0][tile, :]
            ext_grad[tile, :] = part


def output_kernel(count, weights, gathered, output):
    result = matmul(weights[...].reshape(KV * C, C), gathered[...], ((0,), (0,)))
    output[...] = masked(count, result.T).astype(bf16)


def finish_kernel(count, ext_grad, for_upper, for_lower, send, grad_features):
    total = ext_grad[:VOX, :]
    for side, returned in ((1, for_upper), (0, for_lower)):
        rows = onehot(send[side : side + 1, :], VOX)
        total = total + joined(matmul(rows, split(returned[...])))
    grad_features[...] = masked(count, total).astype(bf16)


def exponents(top):
    return jnp.clip(jnp.floor(jnp.log2(jnp.maximum(top, 1e-37))), -100.0, 100.0)


def steps(values, exponent):
    scaled = jnp.round(values * jnp.exp2(14.0 - exponent))
    return jnp.clip(scaled, -32767.0, 32767.0).astype(jnp.int32)


def encode(values, coded):
    exponent = exponents(jnp.max(jnp.abs(values), axis=0, keepdims=True))
    coded[:QUARTER, :] = steps(values, exponent).astype(jnp.int16)
    exponent = jnp.broadcast_to(exponent, (CODED - QUARTER, C))
    coded[QUARTER:, :] = exponent.astype(jnp.int32).astype(jnp.int16)


def decode(coded):
    values = coded[...].astype(jnp.int32).astype(f32)
    return values[:QUARTER, :] * jnp.exp2(values[QUARTER : QUARTER + 1, :] - 14.0)


def decode_pieces(coded):
    values = coded[...].astype(jnp.int32).astype(f32).reshape(PIECES, 8, C)
    return values * jnp.exp2(values[:, 7:, :] - 14.0)


def halves_kernel(kept, received, quarters):
    for i in range(4):
        rows = slice(i * QUARTER, (i + 1) * QUARTER)
        encode(kept[rows, :] + received[rows, :], quarters.at[i])


def quarters_kernel(quarters, pieces, lines):
    total = sum(decode(quarters.at[i]) for i in range(4))
    total = jnp.concatenate([total, jnp.zeros((7 * PIECES - QUARTER, C), f32)], axis=0)
    parts = [total[j * PIECES : (j + 1) * PIECES, :] for j in range(7)]
    exponent = exponents(functools.reduce(jnp.maximum, [jnp.abs(part) for part in parts]))
    for j, part in enumerate(parts):
        lines[pl.ds(j, PIECES, stride=8), :] = steps(part, exponent)
    lines[pl.ds(7, PIECES, stride=8), :] = exponent.astype(jnp.int32)
    pieces[...] = lines[...].astype(jnp.int16)


def pieces_kernel(pieces, spread):
    total = jnp.sum(decode_pieces(pieces), axis=0)
    last = lax.broadcasted_iota(jnp.int32, total.shape, 0) == 7
    total = jnp.where(last, 0.0, total)
    exponent = exponents(jnp.max(jnp.abs(total), axis=0, keepdims=True))
    coded = jnp.where(last, exponent.astype(jnp.int32), steps(total, exponent))
    coded = jnp.broadcast_to(coded[None], (PIECES, 8, C)).reshape(8 * PIECES, C)
    spread[...] = coded.astype(jnp.int16)


def whole_kernel(kept, received, whole, lines, buffer, sems):
    core = lax.axis_index("c")
    copies = []
    for i, (half, place) in enumerate(((kept, core), (received, 1 - core))):
        for q in range(4):
            lines[4 * i + q] = decode_pieces(half.at[q]).reshape(8 * PIECES, C)
            for j in range(7):
                start = j * PIECES
                count = min(PIECES, QUARTER - start)
                rows = slice(q * QUARTER + start, q * QUARTER + start + count)
                buffer[i, rows, :] = lines[4 * i + q, pl.ds(j, count, stride=8), :]
        rows = pl.ds(pl.multiple_of(place * HALF, 8), HALF)
        copies.append(pltpu.make_async_copy(buffer.at[i], whole.at[rows], sems.at[i]))
        copies[i].start()
    for copy in copies:
        copy.wait()


def call(kernel, name, args, outs, scratch=(), flops=0, scalars=1, space=pltpu.VMEM):
    scalar = pl.BlockSpec(memory_space=pltpu.SMEM)
    vector = pl.BlockSpec(memory_space=pltpu.VMEM)
    operand = pl.BlockSpec(memory_space=space)
    outs = tuple(jax.ShapeDtypeStruct(*o) for o in outs)
    moved = sum(a.size * a.dtype.itemsize for a in (*args, *outs))
    return pl.pallas_call(
        kernel,
        name=name,
        in_specs=[scalar] * scalars + [operand] * (len(args) - scalars),
        out_specs=(vector,) * len(outs),
        out_shape=outs,
        scratch_shapes=[pltpu.VMEM(*s) if isinstance(s, tuple) else s for s in scratch],
        cost_estimate=pl.CostEstimate(flops=flops, transcendentals=0, bytes_accessed=moved),
        compiler_params=pltpu.CompilerParams(vmem_limit_bytes=VMEM_LIMIT),
    )(*args)


def scatter(name, offsets, args):
    return call(
        functools.partial(scatter_kernel, offsets),
        name,
        args,
        [((EXT, C), f32)],
        [((GROUP * VOX, 2 * C), bf16)],
        2 * (offsets[1] - offsets[0]) * VOX * C * (C + 2 * EXT),
        scalars=0,
    )[0]


def across_c(part):
    return lax.ppermute(part, "c", [(0, 1), (1, 0)])


def exchange(pieces, axes):
    return lax.all_to_all(pieces, axes, 0, 0, tiled=False)


def per_device(features, weights, kernel_map, send_rows, counts, cotangent):
    features, send, cotangent = features[0], send_rows[0], cotangent[0]
    kernel_map = kernel_map.transpose(1, 0, 2)
    space = ("z", "y")
    size = lax.axis_size(space)
    up = [(i, i + 1) for i in range(size - 1)]
    down = [(i + 1, i) for i in range(size - 1)]
    rows = ((HALO, C), bf16)
    to_lower, to_upper, table, kernel_map = call(
        pick_kernel,
        "pick",
        (counts, *(pltpu.with_memory_space_constraint(a, pltpu.HBM) for a in (features, send, kernel_map))),
        [rows, rows, ((C, VOX), bf16), ((KV, 1, VOX), jnp.int32)],
        [((VOX, C), bf16), ((2, HALO), jnp.int32), pltpu.SemaphoreType.DMA((3,))],
        space=pltpu.HBM,
    )
    lower_in = lax.ppermute(to_upper, space, up)
    upper_in = lax.ppermute(to_lower, space, down)
    (own,) = call(
        local_kernel,
        "local",
        (table, kernel_map),
        [((KV * C, VOX), bf16)],
        flops=2 * KV * VOX * C * VOX,
        scalars=0,
    )
    kept, sent, gathered, grad_rows = call(
        halo_kernel,
        "halo",
        (counts, lower_in, upper_in, kernel_map, own, cotangent),
        [((HALF, C), f32), ((HALF, C), f32), ((KV * C, VOX), bf16), ((VOX, C), bf16)],
        [((C, 2 * HALO), bf16)],
        2 * KV * VOX * C * (2 * HALO + C),
    )
    received = across_c(sent)
    (output,) = call(
        output_kernel,
        "output",
        (counts, weights, gathered),
        [((VOX, C), bf16)],
        flops=2 * KV * VOX * C * C,
    )
    ext_grad = scatter("scatter_first", (0, FIRST), (grad_rows, weights, kernel_map))
    received, ext_grad, output = lax.optimization_barrier((received, ext_grad, output))
    coded = ((4, CODED, C), jnp.int16)
    (quarters,) = call(halves_kernel, "halves", (kept, received), [coded], scalars=0)
    quarters = exchange(quarters, "x")
    ext_grad = scatter("scatter_rest", (FIRST, KV), (grad_rows, weights, kernel_map, ext_grad))
    quarters, ext_grad = lax.optimization_barrier((quarters, ext_grad))
    dealt = ((8 * PIECES, C), jnp.int16)
    (pieces,) = call(
        quarters_kernel,
        "quarters",
        (quarters,),
        [dealt],
        [((8 * PIECES, C), jnp.int32)],
        scalars=0,
    )
    pieces = exchange(pieces.reshape(PIECES, 8, C), space)
    for_lower = lax.ppermute(ext_grad[VOX + HALO :], space, up)
    for_upper = lax.ppermute(ext_grad[VOX : VOX + HALO], space, down)
    pieces, for_lower, for_upper = lax.optimization_barrier((pieces, for_lower, for_upper))
    pieces = pieces.reshape(8 * PIECES, C)
    (pieces,) = call(pieces_kernel, "pieces", (pieces,), [dealt], scalars=0)
    quarter = exchange(pieces.reshape(PIECES, 8, C), space).reshape(8 * PIECES, C)
    half = exchange(jnp.broadcast_to(quarter[None], (4, 8 * PIECES, C)), "x")
    half, ext_grad = lax.optimization_barrier((half, ext_grad))
    received = across_c(half)
    (grad_features,) = call(
        finish_kernel,
        "finish",
        (counts, ext_grad, for_upper, for_lower, send),
        [((VOX, C), bf16)],
    )
    received, grad_features = lax.optimization_barrier((received, grad_features))
    grad_weights = pl.pallas_call(
        whole_kernel,
        name="whole",
        in_specs=[pl.BlockSpec(memory_space=pltpu.VMEM)] * 2,
        out_specs=pl.BlockSpec(memory_space=pl.ANY),
        out_shape=jax.ShapeDtypeStruct((KV * C, C), f32),
        scratch_shapes=[
            pltpu.VMEM((8, 8 * PIECES, C), f32),
            pltpu.VMEM((2, HALF, C), f32),
            pltpu.SemaphoreType.DMA((2,)),
        ],
        compiler_params=pltpu.CompilerParams(vmem_limit_bytes=8 * 2**20),
    )(half, received).reshape(KV, C, C)
    return output[None], grad_features[None], grad_weights


def solution(mesh):
    fine = Mesh(mesh.devices.reshape(8, 8, 4, 2), ("z", "y", "x", "c"))
    space, batch = ("z", "y"), ("x", "c")
    in_specs = (
        P(batch, space, None),
        P(),
        P(batch, None, space),
        P(batch, None, space),
        P(batch, space),
        P(batch, space, None),
    )
    out_specs = (P(batch, space, None), P(batch, space, None), P())
    return jax.shard_map(
        per_device, mesh=fine, in_specs=in_specs, out_specs=out_specs, check_vma=False
    )
```

```python
import functools

import jax
import jax.numpy as jnp
from jax import lax
from jax.experimental import pallas as pl
from jax.experimental.pallas import tpu as pltpu
from jax.sharding import Mesh, PartitionSpec as P

C = 128
KV = 27
VOX = 512
HALO = 128
EXT = VOX + 2 * HALO
SCALE = 262144**-0.5
HALF = KV * C // 2
QUARTER = HALF // 4
CODED = QUARTER + 16
PIECES = 64
GROUP = 3
FIRST = 3
TILE = 256
VMEM_LIMIT = 16 * 2**20

f32 = jnp.float32
bf16 = jnp.bfloat16


def onehot(indices, rows, first=0):
    line = lax.broadcasted_iota(jnp.int32, (rows, indices.shape[1]), 0) + first
    return jnp.where(line == indices, jnp.ones((), bf16), jnp.zeros((), bf16))


def offset_onehot(kernel_map, k, rows, first=0):
    return onehot(kernel_map[k], rows, first)


def masked(count, values):
    alive = lax.broadcasted_iota(jnp.int32, values.shape, 0) < count[0, 0]
    return jnp.where(alive, values, jnp.zeros((), values.dtype))


def split(values):
    high = values.astype(bf16)
    low = (values - high.astype(f32)).astype(bf16)
    return jnp.concatenate([high, low], axis=1)


def joined(both):
    return both[:, :C] + both[:, C:]


def matmul(a, b, dims=((1,), (0,))):
    return lax.dot_general(a, b, (dims, ((), ())), preferred_element_type=f32)


def pick_kernel(
    count, features, send, kernel_map, to_lower, to_upper, table, kernel_map_out, rows, lists, sems
):
    copies = [
        pltpu.make_async_copy(source, target, sems.at[i])
        for i, (source, target) in enumerate(
            ((features, rows), (send, lists), (kernel_map, kernel_map_out))
        )
    ]
    for copy in copies:
        copy.start()
    for copy in copies:
        copy.wait()
    live = masked(count, rows[...])
    for side, outgoing in ((0, to_lower), (1, to_upper)):
        picked = onehot(lists[side : side + 1, :], VOX)
        outgoing[...] = matmul(picked, live, ((0,), (0,))).astype(bf16)
    table[...] = live.T


def local_kernel(table, kernel_map, gathered):
    for k in range(KV):
        rows = offset_onehot(kernel_map, k, VOX)
        gathered[k * C : (k + 1) * C, :] = matmul(table[...], rows).astype(bf16)


def halo_kernel(
    count, lower, upper, kernel_map, own, cotangent, kept, sent, gathered, grad_rows, table
):
    table[:, :HALO] = lower[...].T
    table[:, HALO:] = upper[...].T
    grad_rows[...] = masked(count, cotangent[...])
    for k in range(KV):
        rows = offset_onehot(kernel_map, k, 2 * HALO, VOX)
        part = slice(k * C, (k + 1) * C)
        gathered[part, :] = own[part, :] + matmul(table[...], rows).astype(bf16)
    first_core = lax.axis_index("c") == 0
    for row in range(0, HALF, HALF // 9):
        parts = [slice(row + start, row + start + HALF // 9) for start in (0, HALF)]
        low, high = (matmul(gathered[part, :], grad_rows[...]) * SCALE for part in parts)
        kept[parts[0], :] = jnp.where(first_core, low, high)
        sent[parts[0], :] = jnp.where(first_core, high, low)


def scatter_kernel(offsets, grad_rows, weights, kernel_map, *refs):
    *earlier, ext_grad, contribs = refs
    for first in range(*offsets, GROUP):
        group = range(first, first + GROUP)
        for j, k in enumerate(group):
            contrib = matmul(grad_rows[...], weights[k], ((1,), (1,)))
            contribs[j * VOX : (j + 1) * VOX, :] = split(contrib)
        for row in range(0, EXT, TILE):
            rows = [offset_onehot(kernel_map, k, TILE, row) for k in group]
            part = joined(matmul(jnp.concatenate(rows, axis=1), contribs[...]))
            tile = slice(row, row + TILE)
            if first > offsets[0]:
                part += ext_grad[tile, :]
            elif earlier:
                part += earlier[0][tile, :]
            ext_grad[tile, :] = part


def output_kernel(count, weights, gathered, output):
    result = matmul(weights[...].reshape(KV * C, C), gathered[...], ((0,), (0,)))
    output[...] = masked(count, result.T).astype(bf16)


def finish_kernel(count, ext_grad, for_upper, for_lower, send, grad_features):
    total = ext_grad[:VOX, :]
    for side, returned in ((1, for_upper), (0, for_lower)):
        rows = onehot(send[side : side + 1, :], VOX)
        total = total + joined(matmul(rows, split(returned[...])))
    grad_features[...] = masked(count, total).astype(bf16)


def exponents(top):
    return jnp.clip(jnp.floor(jnp.log2(jnp.maximum(top, 1e-37))), -100.0, 100.0)


def steps(values, exponent):
    scaled = jnp.round(values * jnp.exp2(14.0 - exponent))
    return jnp.clip(scaled, -32767.0, 32767.0).astype(jnp.int32)


def encode(values, coded):
    exponent = exponents(jnp.max(jnp.abs(values), axis=0, keepdims=True))
    coded[:QUARTER, :] = steps(values, exponent).astype(jnp.int16)
    exponent = jnp.broadcast_to(exponent, (CODED - QUARTER, C))
    coded[QUARTER:, :] = exponent.astype(jnp.int32).astype(jnp.int16)


def decode(coded):
    values = coded[...].astype(jnp.int32).astype(f32)
    return values[:QUARTER, :] * jnp.exp2(values[QUARTER : QUARTER + 1, :] - 14.0)


def decode_pieces(coded):
    values = coded[...].astype(jnp.int32).astype(f32).reshape(PIECES, 8, C)
    return values * jnp.exp2(values[:, 7:, :] - 14.0)


def halves_kernel(kept, received, quarters):
    for i in range(4):
        rows = slice(i * QUARTER, (i + 1) * QUARTER)
        encode(kept[rows, :] + received[rows, :], quarters.at[i])


def quarters_kernel(quarters, pieces, lines):
    total = sum(decode(quarters.at[i]) for i in range(4))
    total = jnp.concatenate([total, jnp.zeros((7 * PIECES - QUARTER, C), f32)], axis=0)
    parts = [total[j * PIECES : (j + 1) * PIECES, :] for j in range(7)]
    exponent = exponents(functools.reduce(jnp.maximum, [jnp.abs(part) for part in parts]))
    for j, part in enumerate(parts):
        lines[pl.ds(j, PIECES, stride=8), :] = steps(part, exponent)
    lines[pl.ds(7, PIECES, stride=8), :] = exponent.astype(jnp.int32)
    pieces[...] = lines[...].astype(jnp.int16)


def pieces_kernel(pieces, spread):
    total = jnp.sum(decode_pieces(pieces), axis=0)
    last = lax.broadcasted_iota(jnp.int32, total.shape, 0) == 7
    total = jnp.where(last, 0.0, total)
    exponent = exponents(jnp.max(jnp.abs(total), axis=0, keepdims=True))
    coded = jnp.where(last, exponent.astype(jnp.int32), steps(total, exponent))
    coded = jnp.broadcast_to(coded[None], (PIECES, 8, C)).reshape(8 * PIECES, C)
    spread[...] = coded.astype(jnp.int16)


def whole_kernel(kept, received, whole, lines, buffer, sems):
    core = lax.axis_index("c")
    copies = []
    for i, (half, place) in enumerate(((kept, core), (received, 1 - core))):
        for q in range(4):
            lines[4 * i + q] = decode_pieces(half.at[q]).reshape(8 * PIECES, C)
            for j in range(7):
                start = j * PIECES
                count = min(PIECES, QUARTER - start)
                rows = slice(q * QUARTER + start, q * QUARTER + start + count)
                buffer[i, rows, :] = lines[4 * i + q, pl.ds(j, count, stride=8), :]
        rows = pl.ds(pl.multiple_of(place * HALF, 8), HALF)
        copies.append(pltpu.make_async_copy(buffer.at[i], whole.at[rows], sems.at[i]))
        copies[i].start()
    for copy in copies:
        copy.wait()


def call(kernel, name, args, outs, scratch=(), flops=0, scalars=1, space=pltpu.VMEM):
    scalar = pl.BlockSpec(memory_space=pltpu.SMEM)
    vector = pl.BlockSpec(memory_space=pltpu.VMEM)
    operand = pl.BlockSpec(memory_space=space)
    outs = tuple(jax.ShapeDtypeStruct(*o) for o in outs)
    moved = sum(a.size * a.dtype.itemsize for a in (*args, *outs))
    return pl.pallas_call(
        kernel,
        name=name,
        in_specs=[scalar] * scalars + [operand] * (len(args) - scalars),
        out_specs=(vector,) * len(outs),
        out_shape=outs,
        scratch_shapes=[pltpu.VMEM(*s) if isinstance(s, tuple) else s for s in scratch],
        cost_estimate=pl.CostEstimate(flops=flops, transcendentals=0, bytes_accessed=moved),
        compiler_params=pltpu.CompilerParams(vmem_limit_bytes=VMEM_LIMIT),
    )(*args)


def scatter(name, offsets, args):
    return call(
        functools.partial(scatter_kernel, offsets),
        name,
        args,
        [((EXT, C), f32)],
        [((GROUP * VOX, 2 * C), bf16)],
        2 * (offsets[1] - offsets[0]) * VOX * C * (C + 2 * EXT),
        scalars=0,
    )[0]


def across_c(part):
    return lax.ppermute(part, "c", [(0, 1), (1, 0)])


def exchange(pieces, axes):
    return lax.all_to_all(pieces, axes, 0, 0, tiled=False)


def per_device(features, weights, kernel_map, send_rows, counts, cotangent):
    features, send, cotangent = features[0], send_rows[0], cotangent[0]
    kernel_map = kernel_map.transpose(1, 0, 2)
    space = ("z", "y")
    size = lax.axis_size(space)
    up = [(i, i + 1) for i in range(size - 1)]
    down = [(i + 1, i) for i in range(size - 1)]
    rows = ((HALO, C), bf16)
    to_lower, to_upper, table, kernel_map = call(
        pick_kernel,
        "pick",
        (counts, *(pltpu.with_memory_space_constraint(a, pltpu.HBM) for a in (features, send, kernel_map))),
        [rows, rows, ((C, VOX), bf16), ((KV, 1, VOX), jnp.int32)],
        [((VOX, C), bf16), ((2, HALO), jnp.int32), pltpu.SemaphoreType.DMA((3,))],
        space=pltpu.HBM,
    )
    lower_in = lax.ppermute(to_upper, space, up)
    upper_in = lax.ppermute(to_lower, space, down)
    (own,) = call(
        local_kernel,
        "local",
        (table, kernel_map),
        [((KV * C, VOX), bf16)],
        flops=2 * KV * VOX * C * VOX,
        scalars=0,
    )
    kept, sent, gathered, grad_rows = call(
        halo_kernel,
        "halo",
        (counts, lower_in, upper_in, kernel_map, own, cotangent),
        [((HALF, C), f32), ((HALF, C), f32), ((KV * C, VOX), bf16), ((VOX, C), bf16)],
        [((C, 2 * HALO), bf16)],
        2 * KV * VOX * C * (2 * HALO + C),
    )
    received = across_c(sent)
    (output,) = call(
        output_kernel,
        "output",
        (counts, weights, gathered),
        [((VOX, C), bf16)],
        flops=2 * KV * VOX * C * C,
    )
    ext_grad = scatter("scatter_first", (0, FIRST), (grad_rows, weights, kernel_map))
    received, ext_grad, output = lax.optimization_barrier((received, ext_grad, output))
    coded = ((4, CODED, C), jnp.int16)
    (quarters,) = call(halves_kernel, "halves", (kept, received), [coded], scalars=0)
    quarters = exchange(quarters, "x")
    ext_grad = scatter("scatter_rest", (FIRST, KV), (grad_rows, weights, kernel_map, ext_grad))
    quarters, ext_grad = lax.optimization_barrier((quarters, ext_grad))
    dealt = ((8 * PIECES, C), jnp.int16)
    (pieces,) = call(
        quarters_kernel,
        "quarters",
        (quarters,),
        [dealt],
        [((8 * PIECES, C), jnp.int32)],
        scalars=0,
    )
    pieces = exchange(pieces.reshape(PIECES, 8, C), space)
    pieces, ext_grad = lax.optimization_barrier((pieces, ext_grad))
    pieces = pieces.reshape(8 * PIECES, C)
    (pieces,) = call(pieces_kernel, "pieces", (pieces,), [dealt], scalars=0)
    quarter = exchange(pieces.reshape(PIECES, 8, C), space).reshape(8 * PIECES, C)
    for_lower = lax.ppermute(ext_grad[VOX + HALO :], space, up)
    for_upper = lax.ppermute(ext_grad[VOX : VOX + HALO], space, down)
    quarter, for_lower, for_upper = lax.optimization_barrier((quarter, for_lower, for_upper))
    half = exchange(jnp.broadcast_to(quarter[None], (4, 8 * PIECES, C)), "x")
    half, ext_grad = lax.optimization_barrier((half, ext_grad))
    received = across_c(half)
    (grad_features,) = call(
        finish_kernel,
        "finish",
        (counts, ext_grad, for_upper, for_lower, send),
        [((VOX, C), bf16)],
    )
    received, grad_features = lax.optimization_barrier((received, grad_features))
    grad_weights = pl.pallas_call(
        whole_kernel,
        name="whole",
        in_specs=[pl.BlockSpec(memory_space=pltpu.VMEM)] * 2,
        out_specs=pl.BlockSpec(memory_space=pl.ANY),
        out_shape=jax.ShapeDtypeStruct((KV * C, C), f32),
        scratch_shapes=[
            pltpu.VMEM((8, 8 * PIECES, C), f32),
            pltpu.VMEM((2, HALF, C), f32),
            pltpu.SemaphoreType.DMA((2,)),
        ],
        compiler_params=pltpu.CompilerParams(vmem_limit_bytes=8 * 2**20),
    )(half, received).reshape(KV, C, C)
    return output[None], grad_features[None], grad_weights


def solution(mesh):
    fine = Mesh(mesh.devices.reshape(8, 8, 4, 2), ("z", "y", "x", "c"))
    space, batch = ("z", "y"), ("x", "c")
    in_specs = (
        P(batch, space, None),
        P(),
        P(batch, None, space),
        P(batch, None, space),
        P(batch, space),
        P(batch, space, None),
    )
    out_specs = (P(batch, space, None), P(batch, space, None), P())
    return jax.shard_map(
        per_device, mesh=fine, in_specs=in_specs, out_specs=out_specs, check_vma=False
    )
```

```python
import functools

import jax
import jax.numpy as jnp
from jax import lax
from jax.experimental import pallas as pl
from jax.experimental.pallas import tpu as pltpu
from jax.sharding import Mesh, PartitionSpec as P

C = 128
KV = 27
VOX = 512
HALO = 128
EXT = VOX + 2 * HALO
SCALE = 262144**-0.5
HALF = KV * C // 2
QUARTER = HALF // 4
CODED = QUARTER + 16
PIECES = 64
GROUP = 3
FIRST = 3
TILE = 256
VMEM_LIMIT = 16 * 2**20

f32 = jnp.float32
bf16 = jnp.bfloat16


def onehot(indices, rows, first=0):
    line = lax.broadcasted_iota(jnp.int32, (rows, indices.shape[1]), 0) + first
    return jnp.where(line == indices, jnp.ones((), bf16), jnp.zeros((), bf16))


def offset_onehot(kernel_map, k, rows, first=0):
    return onehot(kernel_map[k], rows, first)


def masked(count, values):
    alive = lax.broadcasted_iota(jnp.int32, values.shape, 0) < count[0, 0]
    return jnp.where(alive, values, jnp.zeros((), values.dtype))


def split(values):
    high = values.astype(bf16)
    low = (values - high.astype(f32)).astype(bf16)
    return jnp.concatenate([high, low], axis=1)


def joined(both):
    return both[:, :C] + both[:, C:]


def matmul(a, b, dims=((1,), (0,))):
    return lax.dot_general(a, b, (dims, ((), ())), preferred_element_type=f32)


def pick_kernel(
    count, features, send, kernel_map, to_lower, to_upper, table, kernel_map_out, rows, lists, sems
):
    copies = [
        pltpu.make_async_copy(source, target, sems.at[i])
        for i, (source, target) in enumerate(
            ((features, rows), (send, lists), (kernel_map, kernel_map_out))
        )
    ]
    for copy in copies:
        copy.start()
    for copy in copies:
        copy.wait()
    live = masked(count, rows[...])
    for side, outgoing in ((0, to_lower), (1, to_upper)):
        picked = onehot(lists[side : side + 1, :], VOX)
        outgoing[...] = matmul(picked, live, ((0,), (0,))).astype(bf16)
    table[...] = live.T


def local_kernel(table, kernel_map, gathered):
    for k in range(KV):
        rows = offset_onehot(kernel_map, k, VOX)
        gathered[k * C : (k + 1) * C, :] = matmul(table[...], rows).astype(bf16)


def halo_kernel(
    count, lower, upper, kernel_map, own, cotangent, kept, sent, gathered, grad_rows, table
):
    table[:, :HALO] = lower[...].T
    table[:, HALO:] = upper[...].T
    grad_rows[...] = masked(count, cotangent[...])
    for k in range(KV):
        rows = offset_onehot(kernel_map, k, 2 * HALO, VOX)
        part = slice(k * C, (k + 1) * C)
        gathered[part, :] = own[part, :] + matmul(table[...], rows).astype(bf16)
    first_core = lax.axis_index("c") == 0
    for row in range(0, HALF, HALF // 9):
        parts = [slice(row + start, row + start + HALF // 9) for start in (0, HALF)]
        low, high = (matmul(gathered[part, :], grad_rows[...]) * SCALE for part in parts)
        kept[parts[0], :] = jnp.where(first_core, low, high)
        sent[parts[0], :] = jnp.where(first_core, high, low)


def scatter_kernel(offsets, grad_rows, weights, kernel_map, *refs):
    *earlier, ext_grad, contribs = refs
    for first in range(*offsets, GROUP):
        group = range(first, first + GROUP)
        for j, k in enumerate(group):
            contrib = matmul(grad_rows[...], weights[k], ((1,), (1,)))
            contribs[j * VOX : (j + 1) * VOX, :] = split(contrib)
        for row in range(0, EXT, TILE):
            rows = [offset_onehot(kernel_map, k, TILE, row) for k in group]
            part = joined(matmul(jnp.concatenate(rows, axis=1), contribs[...]))
            tile = slice(row, row + TILE)
            if first > offsets[0]:
                part += ext_grad[tile, :]
            elif earlier:
                part += earlier[0][tile, :]
            ext_grad[tile, :] = part


def output_kernel(count, weights, gathered, output):
    result = matmul(weights[...].reshape(KV * C, C), gathered[...], ((0,), (0,)))
    output[...] = masked(count, result.T).astype(bf16)


def finish_kernel(count, ext_grad, for_upper, for_lower, send, grad_features):
    total = ext_grad[:VOX, :]
    for side, returned in ((1, for_upper), (0, for_lower)):
        rows = onehot(send[side : side + 1, :], VOX)
        total = total + joined(matmul(rows, split(returned[...])))
    grad_features[...] = masked(count, total).astype(bf16)


def exponents(top):
    return jnp.clip(jnp.floor(jnp.log2(jnp.maximum(top, 1e-37))), -100.0, 100.0)


def steps(values, exponent):
    scaled = jnp.round(values * jnp.exp2(14.0 - exponent))
    return jnp.clip(scaled, -32767.0, 32767.0).astype(jnp.int32)


def encode(values, coded):
    exponent = exponents(jnp.max(jnp.abs(values), axis=0, keepdims=True))
    coded[:QUARTER, :] = steps(values, exponent).astype(jnp.int16)
    exponent = jnp.broadcast_to(exponent, (CODED - QUARTER, C))
    coded[QUARTER:, :] = exponent.astype(jnp.int32).astype(jnp.int16)


def decode(coded):
    values = coded[...].astype(jnp.int32).astype(f32)
    return values[:QUARTER, :] * jnp.exp2(values[QUARTER : QUARTER + 1, :] - 14.0)


def decode_pieces(coded):
    values = coded[...].astype(jnp.int32).astype(f32).reshape(PIECES, 8, C)
    return values * jnp.exp2(values[:, 7:, :] - 14.0)


def halves_kernel(kept, received, quarters):
    for i in range(4):
        rows = slice(i * QUARTER, (i + 1) * QUARTER)
        encode(kept[rows, :] + received[rows, :], quarters.at[i])


def quarters_kernel(quarters, pieces, lines):
    total = sum(decode(quarters.at[i]) for i in range(4))
    total = jnp.concatenate([total, jnp.zeros((7 * PIECES - QUARTER, C), f32)], axis=0)
    parts = [total[j * PIECES : (j + 1) * PIECES, :] for j in range(7)]
    exponent = exponents(functools.reduce(jnp.maximum, [jnp.abs(part) for part in parts]))
    for j, part in enumerate(parts):
        lines[pl.ds(j, PIECES, stride=8), :] = steps(part, exponent)
    lines[pl.ds(7, PIECES, stride=8), :] = exponent.astype(jnp.int32)
    pieces[...] = lines[: 8 * PIECES, :].astype(jnp.int16)


def pieces_kernel(pieces, spread):
    total = jnp.sum(decode_pieces(pieces), axis=0)
    last = lax.broadcasted_iota(jnp.int32, total.shape, 0) == 7
    total = jnp.where(last, 0.0, total)
    exponent = exponents(jnp.max(jnp.abs(total), axis=0, keepdims=True))
    coded = jnp.where(last, exponent.astype(jnp.int32), steps(total, exponent))
    coded = jnp.broadcast_to(coded[None], (PIECES, 8, C)).reshape(8 * PIECES, C)
    spread[...] = coded.astype(jnp.int16)


def whole_kernel(kept, received, whole, lines, buffer, sems):
    core = lax.axis_index("c")
    copies = []
    for i, (half, place) in enumerate(((kept, core), (received, 1 - core))):
        for q in range(4):
            lines[4 * i + q, : 8 * PIECES, :] = decode_pieces(half.at[q]).reshape(8 * PIECES, C)
            for j in range(7):
                start = j * PIECES
                count = min(PIECES, QUARTER - start)
                rows = slice(q * QUARTER + start, q * QUARTER + start + count)
                buffer[i, rows, :] = lines[4 * i + q, pl.ds(j, count, stride=8), :]
        rows = pl.ds(pl.multiple_of(place * HALF, 8), HALF)
        copies.append(pltpu.make_async_copy(buffer.at[i], whole.at[rows], sems.at[i]))
        copies[i].start()
    for copy in copies:
        copy.wait()


def call(kernel, name, args, outs, scratch=(), flops=0, scalars=1, space=pltpu.VMEM):
    scalar = pl.BlockSpec(memory_space=pltpu.SMEM)
    vector = pl.BlockSpec(memory_space=pltpu.VMEM)
    operand = pl.BlockSpec(memory_space=space)
    outs = tuple(jax.ShapeDtypeStruct(*o) for o in outs)
    moved = sum(a.size * a.dtype.itemsize for a in (*args, *outs))
    return pl.pallas_call(
        kernel,
        name=name,
        in_specs=[scalar] * scalars + [operand] * (len(args) - scalars),
        out_specs=(vector,) * len(outs),
        out_shape=outs,
        scratch_shapes=[pltpu.VMEM(*s) if isinstance(s, tuple) else s for s in scratch],
        cost_estimate=pl.CostEstimate(flops=flops, transcendentals=0, bytes_accessed=moved),
        compiler_params=pltpu.CompilerParams(vmem_limit_bytes=VMEM_LIMIT),
    )(*args)


def scatter(name, offsets, args):
    return call(
        functools.partial(scatter_kernel, offsets),
        name,
        args,
        [((EXT, C), f32)],
        [((GROUP * VOX, 2 * C), bf16)],
        2 * (offsets[1] - offsets[0]) * VOX * C * (C + 2 * EXT),
        scalars=0,
    )[0]


def across_c(part):
    return lax.ppermute(part, "c", [(0, 1), (1, 0)])


def exchange(pieces, axes):
    return lax.all_to_all(pieces, axes, 0, 0, tiled=False)


def per_device(features, weights, kernel_map, send_rows, counts, cotangent):
    features, send, cotangent = features[0], send_rows[0], cotangent[0]
    kernel_map = kernel_map.transpose(1, 0, 2)
    space = ("z", "y")
    size = lax.axis_size(space)
    up = [(i, i + 1) for i in range(size - 1)]
    down = [(i + 1, i) for i in range(size - 1)]
    rows = ((HALO, C), bf16)
    to_lower, to_upper, table, kernel_map = call(
        pick_kernel,
        "pick",
        (counts, *(pltpu.with_memory_space_constraint(a, pltpu.HBM) for a in (features, send, kernel_map))),
        [rows, rows, ((C, VOX), bf16), ((KV, 1, VOX), jnp.int32)],
        [((VOX, C), bf16), ((2, HALO), jnp.int32), pltpu.SemaphoreType.DMA((3,))],
        space=pltpu.HBM,
    )
    lower_in = lax.ppermute(to_upper, space, up)
    upper_in = lax.ppermute(to_lower, space, down)
    (own,) = call(
        local_kernel,
        "local",
        (table, kernel_map),
        [((KV * C, VOX), bf16)],
        flops=2 * KV * VOX * C * VOX,
        scalars=0,
    )
    kept, sent, gathered, grad_rows = call(
        halo_kernel,
        "halo",
        (counts, lower_in, upper_in, kernel_map, own, cotangent),
        [((HALF, C), f32), ((HALF, C), f32), ((KV * C, VOX), bf16), ((VOX, C), bf16)],
        [((C, 2 * HALO), bf16)],
        2 * KV * VOX * C * (2 * HALO + C),
    )
    received = across_c(sent)
    (output,) = call(
        output_kernel,
        "output",
        (counts, weights, gathered),
        [((VOX, C), bf16)],
        flops=2 * KV * VOX * C * C,
    )
    ext_grad = scatter("scatter_first", (0, FIRST), (grad_rows, weights, kernel_map))
    received, ext_grad, output = lax.optimization_barrier((received, ext_grad, output))
    coded = ((4, CODED, C), jnp.int16)
    (quarters,) = call(halves_kernel, "halves", (kept, received), [coded], scalars=0)
    quarters = exchange(quarters, "x")
    ext_grad = scatter("scatter_rest", (FIRST, KV), (grad_rows, weights, kernel_map, ext_grad))
    quarters, ext_grad = lax.optimization_barrier((quarters, ext_grad))
    dealt = ((8 * PIECES, C), jnp.int16)
    (pieces,) = call(
        quarters_kernel,
        "quarters",
        (quarters,),
        [dealt],
        [((8 * PIECES + 8, C), jnp.int32)],
        scalars=0,
    )
    pieces = exchange(pieces.reshape(PIECES, 8, C), space)
    pieces, ext_grad = lax.optimization_barrier((pieces, ext_grad))
    pieces = pieces.reshape(8 * PIECES, C)
    (pieces,) = call(pieces_kernel, "pieces", (pieces,), [dealt], scalars=0)
    quarter = exchange(pieces.reshape(PIECES, 8, C), space).reshape(8 * PIECES, C)
    for_lower = lax.ppermute(ext_grad[VOX + HALO :], space, up)
    for_upper = lax.ppermute(ext_grad[VOX : VOX + HALO], space, down)
    quarter, for_lower, for_upper = lax.optimization_barrier((quarter, for_lower, for_upper))
    half = exchange(jnp.broadcast_to(quarter[None], (4, 8 * PIECES, C)), "x")
    half, ext_grad = lax.optimization_barrier((half, ext_grad))
    received = across_c(half)
    (grad_features,) = call(
        finish_kernel,
        "finish",
        (counts, ext_grad, for_upper, for_lower, send),
        [((VOX, C), bf16)],
    )
    received, grad_features = lax.optimization_barrier((received, grad_features))
    grad_weights = pl.pallas_call(
        whole_kernel,
        name="whole",
        in_specs=[pl.BlockSpec(memory_space=pltpu.VMEM)] * 2,
        out_specs=pl.BlockSpec(memory_space=pl.ANY),
        out_shape=jax.ShapeDtypeStruct((KV * C, C), f32),
        scratch_shapes=[
            pltpu.VMEM((8, 8 * PIECES + 8, C), f32),
            pltpu.VMEM((2, HALF, C), f32),
            pltpu.SemaphoreType.DMA((2,)),
        ],
        compiler_params=pltpu.CompilerParams(vmem_limit_bytes=8 * 2**20),
    )(half, received).reshape(KV, C, C)
    return output[None], grad_features[None], grad_weights


def solution(mesh):
    fine = Mesh(mesh.devices.reshape(8, 8, 4, 2), ("z", "y", "x", "c"))
    space, batch = ("z", "y"), ("x", "c")
    in_specs = (
        P(batch, space, None),
        P(),
        P(batch, None, space),
        P(batch, None, space),
        P(batch, space),
        P(batch, space, None),
    )
    out_specs = (P(batch, space, None), P(batch, space, None), P())
    return jax.shard_map(
        per_device, mesh=fine, in_specs=in_specs, out_specs=out_specs, check_vma=False
    )
```

```python
import functools

import jax
import jax.numpy as jnp
from jax import lax
from jax.experimental import pallas as pl
from jax.experimental.pallas import tpu as pltpu
from jax.sharding import Mesh, PartitionSpec as P

C = 128
KV = 27
VOX = 512
HALO = 128
EXT = VOX + 2 * HALO
SCALE = 262144**-0.5
HALF = KV * C // 2
QUARTER = HALF // 4
CODED = QUARTER + 16
PIECES = 64
GROUP = 3
FIRST = 3
TILE = 256
VMEM_LIMIT = 16 * 2**20

f32 = jnp.float32
bf16 = jnp.bfloat16


def onehot(indices, rows, first=0):
    line = lax.broadcasted_iota(jnp.int32, (rows, indices.shape[1]), 0) + first
    return jnp.where(line == indices, jnp.ones((), bf16), jnp.zeros((), bf16))


def offset_onehot(kernel_map, k, rows, first=0):
    return onehot(kernel_map[k], rows, first)


def masked(count, values):
    alive = lax.broadcasted_iota(jnp.int32, values.shape, 0) < count[0, 0]
    return jnp.where(alive, values, jnp.zeros((), values.dtype))


def split(values):
    high = values.astype(bf16)
    low = (values - high.astype(f32)).astype(bf16)
    return jnp.concatenate([high, low], axis=1)


def joined(both):
    return both[:, :C] + both[:, C:]


def matmul(a, b, dims=((1,), (0,))):
    return lax.dot_general(a, b, (dims, ((), ())), preferred_element_type=f32)


def pick_kernel(
    count, features, send, kernel_map, to_lower, to_upper, table, kernel_map_out, rows, lists, sems
):
    copies = [
        pltpu.make_async_copy(source, target, sems.at[i])
        for i, (source, target) in enumerate(
            ((features, rows), (send, lists), (kernel_map, kernel_map_out))
        )
    ]
    for copy in copies:
        copy.start()
    for copy in copies:
        copy.wait()
    live = masked(count, rows[...])
    for side, outgoing in ((0, to_lower), (1, to_upper)):
        picked = onehot(lists[side : side + 1, :], VOX)
        outgoing[...] = matmul(picked, live, ((0,), (0,))).astype(bf16)
    table[...] = live.T


def local_kernel(table, kernel_map, gathered):
    for k in range(KV):
        rows = offset_onehot(kernel_map, k, VOX)
        gathered[k * C : (k + 1) * C, :] = matmul(table[...], rows).astype(bf16)


def halo_kernel(
    count, lower, upper, kernel_map, own, cotangent, kept, sent, gathered, grad_rows, table
):
    table[:, :HALO] = lower[...].T
    table[:, HALO:] = upper[...].T
    grad_rows[...] = masked(count, cotangent[...])
    for k in range(KV):
        rows = offset_onehot(kernel_map, k, 2 * HALO, VOX)
        part = slice(k * C, (k + 1) * C)
        gathered[part, :] = own[part, :] + matmul(table[...], rows).astype(bf16)
    first_core = lax.axis_index("c") == 0
    for row in range(0, HALF, HALF // 9):
        parts = [slice(row + start, row + start + HALF // 9) for start in (0, HALF)]
        low, high = (matmul(gathered[part, :], grad_rows[...]) * SCALE for part in parts)
        kept[parts[0], :] = jnp.where(first_core, low, high)
        sent[parts[0], :] = jnp.where(first_core, high, low)


def scatter_kernel(offsets, grad_rows, weights, kernel_map, *refs):
    *earlier, ext_grad, contribs = refs
    for first in range(*offsets, GROUP):
        group = range(first, first + GROUP)
        side = weights[first : first + GROUP].reshape(GROUP * C, C)
        contrib = matmul(grad_rows[...], side, ((1,), (1,)))
        for j in range(GROUP):
            contribs[j * VOX : (j + 1) * VOX, :] = split(contrib[:, j * C : (j + 1) * C])
        for row in range(0, EXT, TILE):
            rows = [offset_onehot(kernel_map, k, TILE, row) for k in group]
            part = joined(matmul(jnp.concatenate(rows, axis=1), contribs[...]))
            tile = slice(row, row + TILE)
            if first > offsets[0]:
                part += ext_grad[tile, :]
            elif earlier:
                part += earlier[0][tile, :]
            ext_grad[tile, :] = part


def output_kernel(count, weights, gathered, output):
    result = matmul(weights[...].reshape(KV * C, C), gathered[...], ((0,), (0,)))
    output[...] = masked(count, result.T).astype(bf16)


def finish_kernel(count, ext_grad, for_upper, for_lower, send, grad_features):
    total = ext_grad[:VOX, :]
    for side, returned in ((1, for_upper), (0, for_lower)):
        rows = onehot(send[side : side + 1, :], VOX)
        total = total + joined(matmul(rows, split(returned[...])))
    grad_features[...] = masked(count, total).astype(bf16)


def exponents(top):
    return jnp.clip(jnp.floor(jnp.log2(jnp.maximum(top, 1e-37))), -100.0, 100.0)


def steps(values, exponent):
    scaled = jnp.round(values * jnp.exp2(14.0 - exponent))
    return jnp.clip(scaled, -32767.0, 32767.0).astype(jnp.int32)


def encode(values, coded):
    exponent = exponents(jnp.max(jnp.abs(values), axis=0, keepdims=True))
    coded[:QUARTER, :] = steps(values, exponent).astype(jnp.int16)
    exponent = jnp.broadcast_to(exponent, (CODED - QUARTER, C))
    coded[QUARTER:, :] = exponent.astype(jnp.int32).astype(jnp.int16)


def decode(coded):
    values = coded[...].astype(jnp.int32).astype(f32)
    return values[:QUARTER, :] * jnp.exp2(values[QUARTER : QUARTER + 1, :] - 14.0)


def decode_pieces(coded):
    values = coded[...].astype(jnp.int32).astype(f32).reshape(PIECES, 8, C)
    return values * jnp.exp2(values[:, 7:, :] - 14.0)


def halves_kernel(kept, received, quarters):
    for i in range(4):
        rows = slice(i * QUARTER, (i + 1) * QUARTER)
        encode(kept[rows, :] + received[rows, :], quarters.at[i])


def quarters_kernel(quarters, pieces, lines):
    total = sum(decode(quarters.at[i]) for i in range(4))
    total = jnp.concatenate([total, jnp.zeros((7 * PIECES - QUARTER, C), f32)], axis=0)
    parts = [total[j * PIECES : (j + 1) * PIECES, :] for j in range(7)]
    exponent = exponents(functools.reduce(jnp.maximum, [jnp.abs(part) for part in parts]))
    for j, part in enumerate(parts):
        lines[pl.ds(j, PIECES, stride=8), :] = steps(part, exponent)
    lines[pl.ds(7, PIECES, stride=8), :] = exponent.astype(jnp.int32)
    pieces[...] = lines[: 8 * PIECES, :].astype(jnp.int16)


def pieces_kernel(pieces, spread):
    total = jnp.sum(decode_pieces(pieces), axis=0)
    last = lax.broadcasted_iota(jnp.int32, total.shape, 0) == 7
    total = jnp.where(last, 0.0, total)
    exponent = exponents(jnp.max(jnp.abs(total), axis=0, keepdims=True))
    coded = jnp.where(last, exponent.astype(jnp.int32), steps(total, exponent))
    coded = jnp.broadcast_to(coded[None], (PIECES, 8, C)).reshape(8 * PIECES, C)
    spread[...] = coded.astype(jnp.int16)


def whole_kernel(kept, received, whole, lines, buffer, sems):
    core = lax.axis_index("c")
    copies = []
    for i, (half, place) in enumerate(((kept, core), (received, 1 - core))):
        for q in range(4):
            lines[4 * i + q, : 8 * PIECES, :] = decode_pieces(half.at[q]).reshape(8 * PIECES, C)
            for j in range(7):
                start = j * PIECES
                count = min(PIECES, QUARTER - start)
                rows = slice(q * QUARTER + start, q * QUARTER + start + count)
                buffer[i, rows, :] = lines[4 * i + q, pl.ds(j, count, stride=8), :]
        rows = pl.ds(pl.multiple_of(place * HALF, 8), HALF)
        copies.append(pltpu.make_async_copy(buffer.at[i], whole.at[rows], sems.at[i]))
        copies[i].start()
    for copy in copies:
        copy.wait()


def call(kernel, name, args, outs, scratch=(), flops=0, scalars=1, space=pltpu.VMEM):
    scalar = pl.BlockSpec(memory_space=pltpu.SMEM)
    vector = pl.BlockSpec(memory_space=pltpu.VMEM)
    operand = pl.BlockSpec(memory_space=space)
    outs = tuple(jax.ShapeDtypeStruct(*o) for o in outs)
    moved = sum(a.size * a.dtype.itemsize for a in (*args, *outs))
    return pl.pallas_call(
        kernel,
        name=name,
        in_specs=[scalar] * scalars + [operand] * (len(args) - scalars),
        out_specs=(vector,) * len(outs),
        out_shape=outs,
        scratch_shapes=[pltpu.VMEM(*s) if isinstance(s, tuple) else s for s in scratch],
        cost_estimate=pl.CostEstimate(flops=flops, transcendentals=0, bytes_accessed=moved),
        compiler_params=pltpu.CompilerParams(vmem_limit_bytes=VMEM_LIMIT),
    )(*args)


def scatter(name, offsets, args):
    return call(
        functools.partial(scatter_kernel, offsets),
        name,
        args,
        [((EXT, C), f32)],
        [((GROUP * VOX, 2 * C), bf16)],
        2 * (offsets[1] - offsets[0]) * VOX * C * (C + 2 * EXT),
        scalars=0,
    )[0]


def across_c(part):
    return lax.ppermute(part, "c", [(0, 1), (1, 0)])


def exchange(pieces, axes):
    return lax.all_to_all(pieces, axes, 0, 0, tiled=False)


def per_device(features, weights, kernel_map, send_rows, counts, cotangent):
    features, send, cotangent = features[0], send_rows[0], cotangent[0]
    kernel_map = kernel_map.transpose(1, 0, 2)
    space = ("z", "y")
    size = lax.axis_size(space)
    up = [(i, i + 1) for i in range(size - 1)]
    down = [(i + 1, i) for i in range(size - 1)]
    rows = ((HALO, C), bf16)
    to_lower, to_upper, table, kernel_map = call(
        pick_kernel,
        "pick",
        (counts, *(pltpu.with_memory_space_constraint(a, pltpu.HBM) for a in (features, send, kernel_map))),
        [rows, rows, ((C, VOX), bf16), ((KV, 1, VOX), jnp.int32)],
        [((VOX, C), bf16), ((2, HALO), jnp.int32), pltpu.SemaphoreType.DMA((3,))],
        space=pltpu.HBM,
    )
    lower_in = lax.ppermute(to_upper, space, up)
    upper_in = lax.ppermute(to_lower, space, down)
    (own,) = call(
        local_kernel,
        "local",
        (table, kernel_map),
        [((KV * C, VOX), bf16)],
        flops=2 * KV * VOX * C * VOX,
        scalars=0,
    )
    kept, sent, gathered, grad_rows = call(
        halo_kernel,
        "halo",
        (counts, lower_in, upper_in, kernel_map, own, cotangent),
        [((HALF, C), f32), ((HALF, C), f32), ((KV * C, VOX), bf16), ((VOX, C), bf16)],
        [((C, 2 * HALO), bf16)],
        2 * KV * VOX * C * (2 * HALO + C),
    )
    received = across_c(sent)
    (output,) = call(
        output_kernel,
        "output",
        (counts, weights, gathered),
        [((VOX, C), bf16)],
        flops=2 * KV * VOX * C * C,
    )
    ext_grad = scatter("scatter_first", (0, FIRST), (grad_rows, weights, kernel_map))
    received, ext_grad, output = lax.optimization_barrier((received, ext_grad, output))
    coded = ((4, CODED, C), jnp.int16)
    (quarters,) = call(halves_kernel, "halves", (kept, received), [coded], scalars=0)
    quarters = exchange(quarters, "x")
    ext_grad = scatter("scatter_rest", (FIRST, KV), (grad_rows, weights, kernel_map, ext_grad))
    quarters, ext_grad = lax.optimization_barrier((quarters, ext_grad))
    dealt = ((8 * PIECES, C), jnp.int16)
    (pieces,) = call(
        quarters_kernel,
        "quarters",
        (quarters,),
        [dealt],
        [((8 * PIECES + 8, C), jnp.int32)],
        scalars=0,
    )
    pieces = exchange(pieces.reshape(PIECES, 8, C), space)
    pieces, ext_grad = lax.optimization_barrier((pieces, ext_grad))
    pieces = pieces.reshape(8 * PIECES, C)
    (pieces,) = call(pieces_kernel, "pieces", (pieces,), [dealt], scalars=0)
    quarter = exchange(pieces.reshape(PIECES, 8, C), space).reshape(8 * PIECES, C)
    for_lower = lax.ppermute(ext_grad[VOX + HALO :], space, up)
    for_upper = lax.ppermute(ext_grad[VOX : VOX + HALO], space, down)
    quarter, for_lower, for_upper = lax.optimization_barrier((quarter, for_lower, for_upper))
    half = exchange(jnp.broadcast_to(quarter[None], (4, 8 * PIECES, C)), "x")
    half, ext_grad = lax.optimization_barrier((half, ext_grad))
    received = across_c(half)
    (grad_features,) = call(
        finish_kernel,
        "finish",
        (counts, ext_grad, for_upper, for_lower, send),
        [((VOX, C), bf16)],
    )
    received, grad_features = lax.optimization_barrier((received, grad_features))
    grad_weights = pl.pallas_call(
        whole_kernel,
        name="whole",
        in_specs=[pl.BlockSpec(memory_space=pltpu.VMEM)] * 2,
        out_specs=pl.BlockSpec(memory_space=pl.ANY),
        out_shape=jax.ShapeDtypeStruct((KV * C, C), f32),
        scratch_shapes=[
            pltpu.VMEM((8, 8 * PIECES + 8, C), f32),
            pltpu.VMEM((2, HALF, C), f32),
            pltpu.SemaphoreType.DMA((2,)),
        ],
        compiler_params=pltpu.CompilerParams(vmem_limit_bytes=8 * 2**20),
    )(half, received).reshape(KV, C, C)
    return output[None], grad_features[None], grad_weights


def solution(mesh):
    fine = Mesh(mesh.devices.reshape(8, 8, 4, 2), ("z", "y", "x", "c"))
    space, batch = ("z", "y"), ("x", "c")
    in_specs = (
        P(batch, space, None),
        P(),
        P(batch, None, space),
        P(batch, None, space),
        P(batch, space),
        P(batch, space, None),
    )
    out_specs = (P(batch, space, None), P(batch, space, None), P())
    return jax.shard_map(
        per_device, mesh=fine, in_specs=in_specs, out_specs=out_specs, check_vma=False
    )
```
